512 devices in a mesh: seq: 64 (over z, y), head: 8 (over x, core).
Axes of the slice: x: 4, y: 4, z: 16, core: 2. Of those that a mesh axis runs over, the one named last changes fastest.
Arguments:
- queries: bfloat16 [8192, 8192], P('seq', 'head'), may hold values from -6 to 6
- keys: bfloat16 [8192, 8192], P('seq', 'head'), may hold values from -6 to 6
- values: bfloat16 [8192, 8192], P('seq', 'head'), may hold values from -140 to 140
- log_decay: float32 [8192, 64], P('seq', 'head'), may hold values from -1.5 to 0, as said below
- gain: float32 [8192], P('head'), may hold values from 0.25 to 1.75
- cotangent: bfloat16 [8192, 8192], P('seq', 'head'), may hold values from -6 to 6
Outputs:
- normed: bfloat16 [8192, 8192], P('seq', 'head')
- grad_queries: bfloat16 [8192, 8192], P('seq', 'head')
- grad_keys: bfloat16 [8192, 8192], P('seq', 'head')
- grad_values: bfloat16 [8192, 8192], P('seq', 'head')
The draws below stay inside these ranges and needn't reach their ends.
Inputs may be any that keep to these rules, and one draw needn't show every extreme that they name: `log_decay`: negative everywhere.
All inputs are finite; a program needn't handle non-finite values.
Results may differ from the reference program's by a relative error of at most 0.007.
Values sent between devices are 32-bit elements; how exact they have to be, the bound alone decides.
A program may use at most 128 MiB of HBM per device.

```python
import jax
import jax.numpy as jnp
from jax import lax

HEAD_TOTAL = 64
DH = 128
TOK_DEV = 128
TOKEN_TOTAL = 8192


def draw_values(key, part):
    first, second = jax.random.split(key, 2)
    jitter = jax.random.uniform(second, (HEAD_TOTAL,), jnp.float32)
    head_scale = jnp.exp(jnp.log(10.0) * (jnp.arange(HEAD_TOTAL).astype(jnp.float32) + jitter) / HEAD_TOTAL)
    base = jnp.clip(jax.random.normal(first, (TOKEN_TOTAL, HEAD_TOTAL, DH), jnp.float32), -6.0, 6.0)
    return (base * head_scale[None, :, None]).reshape(TOKEN_TOTAL, HEAD_TOTAL * DH).astype(jnp.bfloat16)


def draw_log_decay(key, part):
    segment_pieces = jax.random.split(key, 5)
    share = 0.5
    fast = jax.random.uniform(segment_pieces[0], (HEAD_TOTAL,), jnp.float32) < share
    fast_rate = jax.random.uniform(segment_pieces[1], (HEAD_TOTAL,), jnp.float32, 1.0 / 50.0, 1.0 / 30.0)
    decline_speed = jnp.where(fast, fast_rate, 0.6 / TOKEN_TOTAL)
    blocks = TOKEN_TOTAL // TOK_DEV
    multiplier = jnp.exp(jax.random.uniform(segment_pieces[2], (blocks, HEAD_TOTAL), jnp.float32, jnp.log(0.5), jnp.log(2.0)))
    multiplier = jnp.repeat(multiplier, TOK_DEV, axis=0)
    spike_location = jax.random.randint(segment_pieces[3], (3, HEAD_TOTAL), 0, TOKEN_TOTAL)
    spike_decline = jnp.log(jax.random.uniform(segment_pieces[4], (3, HEAD_TOTAL), jnp.float32, 0.5, 0.8))
    strike_marks = jnp.arange(TOKEN_TOTAL)[:, None, None] == spike_location[None]
    spike_events = jnp.sum(jnp.where(strike_marks, spike_decline[None], 0.0), axis=1)
    return -decline_speed[None, :] * multiplier + spike_events


def block_scale(rng, extent, shards, smallest, top_value):
    factor_of, own = 1.0, jax.random.fold_in(rng, 6)
    for axis_at, shards_of in shards:
        steps = jnp.exp(jax.random.uniform(jax.random.fold_in(own, axis_at), (shards_of,), jnp.float32, smallest / len(shards), top_value / len(shards)))
        factor_of = factor_of * jnp.repeat(steps, extent[axis_at] // shards_of).reshape([-1 if axis == axis_at else 1 for axis in range(len(extent))])
    return factor_of


def noise(rng, dims, deviation, most, pieces=(), held_as=jnp.bfloat16):
    drawn = jax.random.normal(rng, dims, jnp.float32) * deviation
    if len(pieces) > 0:
        drawn = block_scale(rng, dims, pieces, -0.22, 0.18) * drawn
    return jnp.clip(drawn, min=-most, max=most).astype(held_as)


def setup_inputs(seed: int = 0) -> dict:
    streams_of = jax.random.split(jax.random.key(seed), 7)
    queries = noise(streams_of[0], (TOKEN_TOTAL, HEAD_TOTAL * DH), 1.0, 6.0, ((0, 64), (1, 8)))
    keys = noise(streams_of[1], (TOKEN_TOTAL, HEAD_TOTAL * DH), 1.0, 6.0, ((0, 64), (1, 8)))
    values = draw_values(jax.random.fold_in(streams_of[6], 71), 0)
    log_decay = draw_log_decay(jax.random.fold_in(streams_of[6], 71), 0)
    gain = jnp.clip(1.0 + 0.15 * jax.random.normal(streams_of[4], (HEAD_TOTAL * DH,), jnp.float32), 0.25, 1.75)
    cotangent = noise(streams_of[5], (TOKEN_TOTAL, HEAD_TOTAL * DH), 1.0, 6.0, ((0, 64), (1, 8)))
    return {"queries": queries, "keys": keys, "values": values, "log_decay": log_decay, "gain": gain, "cotangent": cotangent}


EPSILON = 1e-05

def rounded(x):
    return lax.optimization_barrier(x.astype(jnp.bfloat16)).astype(jnp.float32)

def decay_table(cumulative):
    by_head = cumulative.T
    gaps = by_head[:, :, None] - by_head[:, None, :]
    count = cumulative.shape[0]
    causal = (jnp.arange(count)[:, None] >= jnp.arange(count)[None, :])[None]
    return jnp.where(causal, jnp.exp(jnp.where(causal, gaps, 0.0)), 0.0)

def reference(queries, keys, values, log_decay, gain, cotangent):
    blocks = TOKEN_TOTAL // TOK_DEV
    scaling = DH ** (-0.5)
    features = HEAD_TOTAL * DH
    shape = (blocks, TOK_DEV, HEAD_TOTAL, DH)
    query_rows = queries.reshape(shape)
    key_rows = keys.reshape(shape)
    value_rows = values.reshape(shape)
    grad_rows = cotangent.reshape(shape)
    cumulative = jnp.cumsum(log_decay.astype(jnp.float32).reshape(blocks, TOK_DEV, HEAD_TOTAL), axis=1)
    totals = cumulative[:, -1]
    gain_rows = gain.astype(jnp.float32).reshape(HEAD_TOTAL, DH)

    def first_pass(item):
        key_part, value_part, cumul = item
        tail = jnp.exp(cumul[-1][None] - cumul)
        keys_decayed = (key_part.astype(jnp.float32) * tail[:, :, None]).astype(jnp.bfloat16)
        state = jnp.einsum('jhd,jhe->hde', keys_decayed.astype(jnp.float32), value_part.astype(jnp.float32))
        return (keys_decayed, state)
    keys_decayed, block_states = lax.map(first_pass, (key_rows, value_rows, cumulative))

    def chain_step(carry, item):
        total, state = item
        return (jnp.exp(total)[:, None, None] * carry + state, carry)
    zero_state = jnp.zeros((HEAD_TOTAL, DH, DH), jnp.float32)
    _, incoming = lax.scan(chain_step, zero_state, (totals, block_states))

    def second_pass(item):
        query_part, key_part, value_part, grad_part, cumul, state = item
        weights = decay_table(cumul) * scaling
        query_f = query_part.astype(jnp.float32)
        key_f = key_part.astype(jnp.float32)
        value_f = value_part.astype(jnp.float32)
        scores = rounded(jnp.einsum('thd,jhd->htj', query_f, key_f) * weights)
        state_b = rounded(state)
        row_scale = scaling * jnp.exp(cumul)
        queried = rounded(query_f * row_scale[:, :, None])
        attended = jnp.einsum('htj,jhd->thd', scores, value_f) + jnp.einsum('thd,hde->the', queried, state_b)
        square_sum = lax.optimization_barrier(jnp.sum(attended * attended, axis=(1, 2)))
        upstream = grad_part.astype(jnp.float32) * gain_rows
        slope_sum = lax.optimization_barrier(jnp.sum(upstream * attended, axis=(1, 2)))
        inverse = lax.rsqrt(square_sum / features + EPSILON)
        normed = (attended * inverse[:, None, None] * gain_rows).astype(jnp.bfloat16)
        grad_out = rounded(inverse[:, None, None] * upstream - attended * (inverse ** 3 * slope_sum / features)[:, None, None])
        grad_scores = rounded(jnp.einsum('the,jhe->htj', grad_out, value_f) * weights)
        grad_query = jnp.einsum('htj,jhd->thd', grad_scores, key_f) + jnp.einsum('the,hde->thd', grad_out, state_b) * row_scale[:, :, None]
        grad_key_local = jnp.einsum('htj,thd->jhd', grad_scores, query_f)
        grad_value_local = jnp.einsum('htj,the->jhe', scores, grad_out)
        grad_state = jnp.einsum('thd,the->hde', queried, grad_out)
        return (normed, grad_query.astype(jnp.bfloat16), grad_key_local, grad_value_local, grad_state)
    normed, grad_queries, grad_key_local, grad_value_local, grad_states = lax.map(second_pass, (query_rows, key_rows, value_rows, grad_rows, cumulative, incoming))
    _, outgoing = lax.scan(chain_step, zero_state, (totals, grad_states), reverse=True)

    def third_pass(item):
        value_part, keys_dec, cumul, key_local, value_local, state = item
        state_b = rounded(state)
        tail = jnp.exp(cumul[-1][None] - cumul)
        grad_key = key_local + jnp.einsum('jhe,hde->jhd', value_part.astype(jnp.float32), state_b) * tail[:, :, None]
        grad_value = value_local + jnp.einsum('jhd,hde->jhe', keys_dec.astype(jnp.float32), state_b)
        return (grad_key.astype(jnp.bfloat16), grad_value.astype(jnp.bfloat16))
    grad_keys, grad_values = lax.map(third_pass, (value_rows, keys_decayed, cumulative, grad_key_local, grad_value_local, outgoing))
    flat = (TOKEN_TOTAL, HEAD_TOTAL * DH)
    return (normed.reshape(flat), grad_queries.reshape(flat), grad_keys.reshape(flat), grad_values.reshape(flat))
```

```python
import jax
import jax.numpy as jnp
from jax import lax
from jax.sharding import PartitionSpec as P

EPSILON = 1e-05


def carried_in(part, axis, reverse):
    total, state = part
    count = lax.axis_size(axis)
    place = lax.axis_index(axis)
    heads = total.shape[0]
    totals = lax.all_gather(total, axis)
    mine = lax.dynamic_index_in_dim(totals, place * heads // count, 1, False)
    at = jnp.arange(count)
    first, last = (at[:, None], at[None, :]) if reverse else (at[None, :], at[:, None])
    between = (at > first[:, :, None]) & (at < last[:, :, None])
    gaps = jnp.sum(jnp.where(between, mine, 0.0), axis=-1)
    decay = jnp.where(first < last, 0.5 * jnp.exp(gaps), 0.0)
    pieces = state.reshape(count, -1, state.shape[-1])
    swapped = lax.all_to_all(pieces, axis, 0, 0, tiled=True)
    summed = jnp.einsum("ab,bcd->acd", decay, swapped, precision=lax.Precision.HIGHEST)
    return 2.0 * lax.all_to_all(summed, axis, 0, 0, tiled=True).reshape(state.shape)


def per_device(queries, keys, values, log_decay, gain, cotangent):
    tokens, row_width = queries.shape
    head_count = log_decay.shape[1]
    head_size = row_width // head_count
    scaling = head_size ** (-0.5)
    features = row_width * lax.axis_size("head")
    shape = (tokens, head_count, head_size)
    query_rows = queries.reshape(shape)
    key_rows = keys.reshape(shape)
    value_rows = values.reshape(shape)
    gain_rows = gain.reshape(head_count, head_size)
    cumulative = jnp.cumsum(log_decay, axis=0)
    block_total = cumulative[-1]
    by_head = cumulative.T
    gaps = by_head[:, :, None] - by_head[:, None, :]
    causal = (
        lax.broadcasted_iota(jnp.int32, (tokens, tokens), 0)
        >= lax.broadcasted_iota(jnp.int32, (tokens, tokens), 1)
    )[None]
    weights = jnp.where(causal, jnp.exp(jnp.where(causal, gaps, 0.0)), 0.0) * scaling
    tail = jnp.exp(block_total[None, :] - cumulative)
    keys_decayed = (key_rows * tail[:, :, None]).astype(jnp.bfloat16)
    block_state = jnp.einsum(
        "jhd,jhe->hde", keys_decayed, value_rows, preferred_element_type=jnp.float32
    )
    incoming = carried_in((block_total, block_state), "seq", False).astype(jnp.bfloat16)
    scores = (
        jnp.einsum("thd,jhd->htj", query_rows, key_rows, preferred_element_type=jnp.float32)
        * weights
    ).astype(jnp.bfloat16)
    row_scale = scaling * jnp.exp(cumulative)
    queried = (query_rows * row_scale[:, :, None]).astype(jnp.bfloat16)
    attended = jnp.einsum("htj,jhd->thd", scores, value_rows, preferred_element_type=jnp.float32)
    attended = attended + jnp.einsum(
        "thd,hde->the", queried, incoming, preferred_element_type=jnp.float32
    )
    upstream = cotangent.reshape(shape) * gain_rows
    square_part = jnp.sum(attended * attended, axis=(1, 2))
    square_sum = lax.psum(square_part, "head")
    inverse = lax.rsqrt(square_sum / features + EPSILON)
    unit_rows = attended * inverse[:, None, None]
    slope_unit = lax.psum(jnp.sum(upstream * unit_rows, axis=(1, 2)), "head")
    grad_out = (
        inverse[:, None, None] * upstream
        - unit_rows * (inverse * slope_unit / features)[:, None, None]
    )
    normed = (
        (attended * inverse[:, None, None] * gain_rows)
        .astype(jnp.bfloat16)
        .reshape(tokens, row_width)
    )
    grad_out = grad_out.astype(jnp.bfloat16)
    grad_state = jnp.einsum("thd,the->hde", queried, grad_out, preferred_element_type=jnp.float32)
    outgoing = carried_in((block_total, grad_state), "seq", True).astype(jnp.bfloat16)
    grad_scores = (
        jnp.einsum("the,jhe->htj", grad_out, value_rows, preferred_element_type=jnp.float32)
        * weights
    ).astype(jnp.bfloat16)
    grad_query = jnp.einsum(
        "htj,jhd->thd", grad_scores, key_rows, preferred_element_type=jnp.float32
    )
    grad_query = (
        grad_query
        + jnp.einsum("the,hde->thd", grad_out, incoming, preferred_element_type=jnp.float32)
        * row_scale[:, :, None]
    )
    grad_key = jnp.einsum(
        "htj,thd->jhd", grad_scores, query_rows, preferred_element_type=jnp.float32
    )
    grad_key = (
        grad_key
        + jnp.einsum("jhe,hde->jhd", value_rows, outgoing, preferred_element_type=jnp.float32)
        * tail[:, :, None]
    )
    grad_value = jnp.einsum("htj,the->jhe", scores, grad_out, preferred_element_type=jnp.float32)
    grad_value = grad_value + jnp.einsum(
        "jhd,hde->jhe", keys_decayed, outgoing, preferred_element_type=jnp.float32
    )
    flat = (tokens, row_width)
    return (
        normed,
        grad_query.astype(jnp.bfloat16).reshape(flat),
        grad_key.astype(jnp.bfloat16).reshape(flat),
        grad_value.astype(jnp.bfloat16).reshape(flat),
    )


def solution(mesh):
    placed = (
        P("seq", "head"),
        P("seq", "head"),
        P("seq", "head"),
        P("seq", "head"),
        P("head"),
        P("seq", "head"),
    )
    return jax.shard_map(
        per_device,
        mesh=mesh,
        in_specs=placed,
        out_specs=(P("seq", "head"), P("seq", "head"), P("seq", "head"), P("seq", "head")),
        check_vma=False,
    )
```

```python
import functools

import jax
import jax.numpy as jnp
from jax import lax
from jax.experimental import pallas as pl
from jax.experimental.pallas import tpu as pltpu
from jax.sharding import PartitionSpec as P

EPSILON = 1e-05
SIDE = 4
F32 = jnp.float32
BF16 = jnp.bfloat16
HIGHEST = lax.Precision.HIGHEST


def dot(a, b, contract, precision=None):
    return lax.dot_general(
        a, b, ((contract[:1], contract[1:]), ((), ())), precision=precision,
        preferred_element_type=F32,
    )


def exchange_order(count):
    return sorted(range(1, count), key=lambda d: -min(d, count - d))


class Exchange:
    def __init__(self, source, target, send_sem, recv_sem, place, count, device, shared=False):
        self.source, self.target, self.place, self.count = source, target, place, count
        self.send_sem, self.recv_sem, self.device, self.shared = send_sem, recv_sem, device, shared
        self.started = []

    def copy(self, peer, slot, step):
        return pltpu.make_async_remote_copy(
            src_ref=self.source if self.shared else self.source.at[peer],
            dst_ref=self.target.at[slot],
            send_sem=self.send_sem.at[step],
            recv_sem=self.recv_sem.at[step],
            device_id=self.device(peer),
            device_id_type=pl.DeviceIdType.MESH,
        )

    def start(self):
        for step in exchange_order(self.count):
            copy = self.copy(lax.rem(self.place + step, self.count), self.place, step)
            copy.start()
            self.started.append(copy)
        self.target[self.place] = self.source[...] if self.shared else self.source[self.place]

    def finish(self):
        for step in range(1, self.count):
            peer = lax.rem(self.place + self.count - step, self.count)
            self.copy(peer, peer, step).wait_recv()

    def drain(self):
        for copy in self.started:
            copy.wait_send()


def kernel(
    seq_count, group, features,
    q_ref, k_ref, v_ref, ld_ref, gain_ref, cot_ref,
    normed_ref, gq_ref, gk_ref, gv_ref,
    w_ref, sc_ref, ds_ref, o_ref, u_ref, gkl_ref, gvl_ref, qd_ref, kd_ref, do_ref, s_ref,
    yb, yrb, zb, zrb, zo, zi, yo, yi,
    yb2, yrb2, zb2, zrb2, zo2, zi2, yo2, yi2,
    hs, hr,
    ys, yr, zs, zr, hs_sem, hr_sem,
):
    tokens = q_ref.shape[0]
    heads = ld_ref.shape[1]
    size = q_ref.shape[1] // heads
    depth = seq_count // SIDE
    own = heads // SIDE
    span = own * size // depth
    scaling = size ** (-0.5)
    seq, head = lax.axis_index("seq"), lax.axis_index("head")
    z, y = seq // SIDE, lax.rem(seq, SIDE)
    def y_peer(p):
        return (z * SIDE + p, head)

    def z_peer(p):
        return (p * SIDE + y, head)

    def h_peer(p):
        return (seq, p)

    barrier = pltpu.get_barrier_semaphore()
    for place, count, device in ((y, SIDE, y_peer), (z, depth, z_peer), (head, group, h_peer)):
        for step in range(1, count):
            pl.semaphore_signal(
                barrier, inc=1, device_id=device(lax.rem(place + step, count)),
                device_id_type=pl.DeviceIdType.MESH,
            )

    def at(h):
        return slice(h * size, (h + 1) * size)

    row = lax.broadcasted_iota(jnp.int32, (tokens, tokens), 0)
    column = lax.broadcasted_iota(jnp.int32, (tokens, tokens), 1)
    causal = row >= column
    lower = jnp.where(causal, 1.0, 0.0).astype(F32)
    log_decay = ld_ref[...]
    c = dot(lower, log_decay, (1, 0), HIGHEST)
    c_rows = dot(log_decay, lower, (0, 1), HIGHEST)
    total = jnp.broadcast_to(c_rows[:, tokens - 1:tokens], (heads, size))
    tail = jnp.exp(c[tokens - 1:tokens, :] - c)
    row_scale = scaling * jnp.exp(c)

    for h in range(heads):
        kd = (k_ref[:, at(h)].astype(F32) * tail[:, h:h + 1]).astype(BF16)
        kd_ref[:, at(h)] = kd
        place = h % own
        yb[h // own, at(place)] = dot(kd, v_ref[:, at(h)], (0, 0))
        yb[h // own, own * size + place * 8:own * size + place * 8 + 8] = jnp.broadcast_to(
            total[h:h + 1], (8, size)
        )
    pl.semaphore_wait(barrier, SIDE + depth + group - 3)

    exchanges = []

    def exchange(source, target, index, sems, place, count, device, shared=False):
        made = Exchange(
            source, target, sems[0].at[index], sems[1].at[index], place, count, device, shared
        )
        made.start()
        exchanges.append(made)
        return made

    def own_total(part, place):
        first = own * size + place * 8
        return yrb[part, first:first + 1]

    def own_decay(part, place):
        return jnp.exp(own_total(part, place))

    moving = exchange(yb, yrb, 0, (ys, yr), y, SIDE, y_peer)
    for h in range(heads):
        gaps = c[:, h:h + 1] - c_rows[h:h + 1, :]
        weights = jnp.where(causal, jnp.exp(jnp.where(causal, gaps, 0.0)), 0.0) * scaling
        w_ref[h] = weights
        sc_ref[h] = (dot(q_ref[:, at(h)], k_ref[:, at(h)], (1, 1)) * weights).astype(BF16)
    moving.finish()
    for place in range(own):
        state = yrb[0, at(place)]
        whole = own_total(0, place)
        for part in range(1, SIDE):
            state = own_decay(part, place) * state + yrb[part, at(place)]
            whole = whole + own_total(part, place)
        slots = slice(place * size // span, (place + 1) * size // span)
        zb[slots, 0:span] = state.reshape(size // span, span, size)
        zb[slots, span:span + 8] = jnp.broadcast_to(whole, (size // span, 8, size))
    moving = exchange(zb, zrb, 0, (zs, zr), z, depth, z_peer)
    for h in range(heads):
        o_ref[:, at(h)] = dot(sc_ref[h], v_ref[:, at(h)], (1, 0))
    moving.finish()
    state = jnp.zeros((span, size), F32)
    for part in range(depth):
        zo[part] = state
        state = jnp.exp(zrb[part, span:span + 1]) * state + zrb[part, 0:span]
    moving = exchange(zo, zi, 1, (zs, zr), z, depth, z_peer)
    for h in range(heads):
        qd_ref[:, at(h)] = (q_ref[:, at(h)].astype(F32) * row_scale[:, h:h + 1]).astype(BF16)
        u_ref[:, at(h)] = cot_ref[:, at(h)].astype(F32) * gain_ref[:, at(h)]
    moving.finish()
    for place in range(own):
        slots = slice(place * size // span, (place + 1) * size // span)
        state = zi[slots].reshape(size, size)
        for part in range(SIDE):
            yo[part, at(place)] = state
            if part < SIDE - 1:
                state = own_decay(part, place) * state + yrb[part, at(place)]
    moving = exchange(yo, yi, 1, (ys, yr), y, SIDE, y_peer)
    moving.finish()

    squares = jnp.zeros((tokens, size), F32)
    slopes = jnp.zeros((tokens, size), F32)
    for h in range(heads):
        state = yi[h // own, at(h % own)].astype(BF16)
        s_ref[h] = state
        o = o_ref[:, at(h)] + dot(qd_ref[:, at(h)], state, (1, 0))
        o_ref[:, at(h)] = o
        squares = squares + o * o
        slopes = slopes + u_ref[:, at(h)] * o
    hs[0:8] = jnp.broadcast_to(jnp.sum(jnp.transpose(squares), axis=0, keepdims=True), (8, tokens))
    hs[8:16] = jnp.broadcast_to(jnp.sum(jnp.transpose(slopes), axis=0, keepdims=True), (8, tokens))
    moving = exchange(hs, hr, 0, (hs_sem, hr_sem), head, group, h_peer, True)
    moving.finish()
    both = hr[0]
    for part in range(1, group):
        both = both + hr[part]
    inverse_row = lax.rsqrt(both[0:1] / features + EPSILON)
    pull_row = inverse_row * inverse_row * (inverse_row * both[8:9]) / features
    inverse = jnp.transpose(jnp.broadcast_to(inverse_row, (size, tokens)))
    pull = jnp.transpose(jnp.broadcast_to(pull_row, (size, tokens)))

    for h in range(heads):
        do = (inverse * u_ref[:, at(h)] - o_ref[:, at(h)] * pull).astype(BF16)
        do_ref[:, at(h)] = do
        yb2[h // own, at(h % own)] = dot(qd_ref[:, at(h)], do, (0, 0))
    moving = exchange(yb2, yrb2, 2, (ys, yr), y, SIDE, y_peer)
    for h in range(heads):
        normed_ref[:, at(h)] = (o_ref[:, at(h)] * inverse * gain_ref[:, at(h)]).astype(BF16)
        ds_ref[h] = (dot(do_ref[:, at(h)], v_ref[:, at(h)], (1, 1)) * w_ref[h]).astype(BF16)
    moving.finish()
    for place in range(own):
        state = yrb2[SIDE - 1, at(place)]
        for part in reversed(range(SIDE - 1)):
            state = own_decay(part, place) * state + yrb2[part, at(place)]
        slots = slice(place * size // span, (place + 1) * size // span)
        zb2[slots] = state.reshape(size // span, span, size)
    moving = exchange(zb2, zrb2, 2, (zs, zr), z, depth, z_peer)
    for h in range(heads):
        gq_ref[:, at(h)] = (
            dot(ds_ref[h], k_ref[:, at(h)], (1, 0))
            + dot(do_ref[:, at(h)], s_ref[h], (1, 1)) * row_scale[:, h:h + 1]
        ).astype(BF16)
    moving.finish()
    state = jnp.zeros((span, size), F32)
    for part in reversed(range(depth)):
        zo2[part] = state
        state = jnp.exp(zrb[part, span:span + 1]) * state + zrb2[part]
    moving = exchange(zo2, zi2, 3, (zs, zr), z, depth, z_peer)
    for h in range(heads):
        gkl_ref[:, at(h)] = dot(ds_ref[h], q_ref[:, at(h)], (0, 0))
        gvl_ref[:, at(h)] = dot(sc_ref[h], do_ref[:, at(h)], (0, 0))
    moving.finish()
    for place in range(own):
        slots = slice(place * size // span, (place + 1) * size // span)
        state = zi2[slots].reshape(size, size)
        for part in reversed(range(SIDE)):
            yo2[part, at(place)] = state
            if part > 0:
                state = own_decay(part, place) * state + yrb2[part, at(place)]
    moving = exchange(yo2, yi2, 3, (ys, yr), y, SIDE, y_peer)
    moving.finish()
    for h in range(heads):
        state = yi2[h // own, at(h % own)].astype(BF16)
        gk_ref[:, at(h)] = (
            gkl_ref[:, at(h)] + dot(v_ref[:, at(h)], state, (1, 1)) * tail[:, h:h + 1]
        ).astype(BF16)
        gv_ref[:, at(h)] = (gvl_ref[:, at(h)] + dot(kd_ref[:, at(h)], state, (1, 0))).astype(BF16)
    for made in exchanges:
        made.drain()


def per_device(queries, keys, values, log_decay, gain, cotangent):
    tokens, width = queries.shape
    heads = log_decay.shape[1]
    size = width // heads
    seq_count, group = lax.axis_size("seq"), lax.axis_size("head")
    depth = seq_count // SIDE
    own = heads // SIDE
    span = own * size // depth
    block = pl.BlockSpec(memory_space=pltpu.VMEM)
    square = (heads, tokens, tokens)
    flat = (tokens, width)
    V = pltpu.VMEM
    with_totals = [
        V((SIDE, own * (size + 8), size), F32), V((SIDE, own * (size + 8), size), F32),
        V((depth, span + 8, size), F32), V((depth, span + 8, size), F32),
    ]
    y_slots, z_slots = V((SIDE, own * size, size), F32), V((depth, span, size), F32)
    back = [z_slots, z_slots, y_slots, y_slots]
    out = jax.ShapeDtypeStruct(flat, BF16)
    return pl.pallas_call(
        functools.partial(kernel, seq_count, group, float(width * group)),
        out_shape=(out, out, out, out),
        in_specs=[block] * 6,
        out_specs=(block,) * 4,
        scratch_shapes=[
            V(square, F32), V(square, BF16), V(square, BF16),
            V(flat, F32), V(flat, F32), V(flat, F32), V(flat, F32),
            V(flat, BF16), V(flat, BF16), V(flat, BF16),
            V((heads, size, size), BF16),
            *with_totals, *back,
            y_slots, y_slots, z_slots, z_slots, *back,
            V((16, tokens), F32), V((group, 16, tokens), F32),
            pltpu.SemaphoreType.DMA((4, SIDE)), pltpu.SemaphoreType.DMA((4, SIDE)),
            pltpu.SemaphoreType.DMA((4, depth)), pltpu.SemaphoreType.DMA((4, depth)),
            pltpu.SemaphoreType.DMA((1, group)), pltpu.SemaphoreType.DMA((1, group)),
        ],
        compiler_params=pltpu.CompilerParams(collective_id=0, has_side_effects=True),
        name="attention_both_ways",
    )(queries, keys, values, log_decay, gain.reshape(1, width), cotangent)


def solution(mesh):
    placed = (
        P("seq", "head"),
        P("seq", "head"),
        P("seq", "head"),
        P("seq", "head"),
        P("head"),
        P("seq", "head"),
    )
    return jax.shard_map(
        per_device,
        mesh=mesh,
        in_specs=placed,
        out_specs=(P("seq", "head"), P("seq", "head"), P("seq", "head"), P("seq", "head")),
        check_vma=False,
    )
```

```python
import functools

import jax
import jax.numpy as jnp
from jax import lax
from jax.experimental import pallas as pl
from jax.experimental.pallas import tpu as pltpu
from jax.sharding import PartitionSpec as P

EPSILON = 1e-05
SIDE = 4
F32 = jnp.float32
BF16 = jnp.bfloat16
HIGHEST = lax.Precision.HIGHEST


def dot(a, b, contract, precision=None):
    return lax.dot_general(
        a, b, ((contract[:1], contract[1:]), ((), ())), precision=precision,
        preferred_element_type=F32,
    )


def exchange_order(count):
    return sorted(range(1, count), key=lambda d: -min(d, count - d))


class Exchange:
    def __init__(self, source, target, send_sem, recv_sem, place, count, device, shared=False):
        self.source, self.target, self.place, self.count = source, target, place, count
        self.send_sem, self.recv_sem, self.device, self.shared = send_sem, recv_sem, device, shared
        self.started = []

    def copy(self, peer, slot, step):
        return pltpu.make_async_remote_copy(
            src_ref=self.source if self.shared else self.source.at[peer],
            dst_ref=self.target.at[slot],
            send_sem=self.send_sem.at[step],
            recv_sem=self.recv_sem.at[step],
            device_id=self.device(peer),
            device_id_type=pl.DeviceIdType.MESH,
        )

    def start(self):
        for step in exchange_order(self.count):
            copy = self.copy(lax.rem(self.place + step, self.count), self.place, step)
            copy.start()
            self.started.append(copy)
        self.target[self.place] = self.source[...] if self.shared else self.source[self.place]

    def finish(self):
        for step in range(1, self.count):
            peer = lax.rem(self.place + self.count - step, self.count)
            self.copy(peer, peer, step).wait_recv()

    def drain(self):
        for copy in self.started:
            copy.wait_send()


def kernel(
    seq_count, group, features,
    q_ref, k_ref, v_ref, ld_ref, gain_ref, cot_ref,
    normed_ref, gq_ref, gk_ref, gv_ref,
    w_ref, sc_ref, ds_ref, o_ref, u_ref, gkl_ref, gvl_ref, qd_ref, kd_ref, do_ref, s_ref,
    yb, yrb, zb, zrb, zo, zi, yo, yi,
    yb2, yrb2, zb2, zrb2, zo2, zi2, yo2, yi2,
    tb, trb, tz, tzr, hs, hr,
    ys, yr, zs, zr, hs_sem, hr_sem,
):
    tokens = q_ref.shape[0]
    heads = ld_ref.shape[0]
    size = q_ref.shape[1] // heads
    depth = seq_count // SIDE
    own = heads // SIDE
    span = size // depth
    scaling = size ** (-0.5)
    seq, head = lax.axis_index("seq"), lax.axis_index("head")
    z, y = seq // SIDE, lax.rem(seq, SIDE)

    def y_peer(p):
        return (z * SIDE + p, head)

    def z_peer(p):
        return (p * SIDE + y, head)

    def h_peer(p):
        return (seq, p)

    barrier = pltpu.get_barrier_semaphore()
    for place, count, device in ((z, depth, z_peer), (y, SIDE, y_peer), (head, group, h_peer)):
        for step in exchange_order(count):
            pl.semaphore_signal(
                barrier, inc=1, device_id=device(lax.rem(place + step, count)),
                device_id_type=pl.DeviceIdType.MESH,
            )

    exchanges = []

    def exchange(source, target, sems, index, place, count, device, shared=False):
        made = Exchange(
            source, target, sems[0].at[index], sems[1].at[index], place, count, device, shared
        )
        made.start()
        exchanges.append(made)
        return made

    def over_y(source, target, index, shared=False):
        return exchange(source, target, (ys, yr), index, y, SIDE, y_peer, shared)

    def over_z(source, target, index, shared=False):
        return exchange(source, target, (zs, zr), index, z, depth, z_peer, shared)

    def at(h):
        return slice(h * size, (h + 1) * size)

    units = range(own)
    in_order = [part * own + unit for unit in units for part in range(SIDE)]
    row = lax.broadcasted_iota(jnp.int32, (tokens, tokens), 0)
    column = lax.broadcasted_iota(jnp.int32, (tokens, tokens), 1)
    causal = row >= column
    lower = jnp.where(causal, 1.0, 0.0).astype(F32)
    log_decay = ld_ref[...]
    c = dot(lower, log_decay, (1, 1), HIGHEST)
    c_rows = dot(log_decay, lower, (1, 1), HIGHEST)
    total = jnp.broadcast_to(c_rows[:, tokens - 1:tokens], (heads, size))
    for part in range(SIDE):
        tb[part] = total[part * own:(part + 1) * own]
    tail = jnp.exp(c[tokens - 1:tokens, :] - c)
    row_scale = scaling * jnp.exp(c)

    for h in in_order:
        kd = (k_ref[:, at(h)].astype(F32) * tail[:, h:h + 1]).astype(BF16)
        kd_ref[:, at(h)] = kd
        yb[h % own, h // own] = dot(kd, v_ref[:, at(h)], (0, 0))
    pl.semaphore_wait(barrier, SIDE + depth + group - 3)

    totals = over_y(tb, trb, 0)
    moving = [over_y(yb.at[unit], yrb.at[unit], 1 + unit) for unit in units]
    totals.finish()
    whole = trb[0]
    for part in range(1, SIDE):
        whole = whole + trb[part]
    tz[...] = whole
    wholes = over_z(tz, tzr, 0, True)

    def own_decay(part, unit):
        return jnp.exp(trb[part, unit:unit + 1])

    for h in in_order:
        gaps = c[:, h:h + 1] - c_rows[h:h + 1, :]
        weights = jnp.where(causal, jnp.exp(jnp.where(causal, gaps, 0.0)), 0.0) * scaling
        w_ref[h] = weights
        sc_ref[h] = (dot(q_ref[:, at(h)], k_ref[:, at(h)], (1, 1)) * weights).astype(BF16)
    out = []
    for unit in units:
        moving[unit].finish()
        state = yrb[unit, 0]
        for part in range(1, SIDE):
            state = own_decay(part, unit) * state + yrb[unit, part]
        zb[unit] = state.reshape(depth, span, size)
        out.append(over_z(zb.at[unit], zrb.at[unit], 1 + unit))
    for h in in_order:
        o_ref[:, at(h)] = dot(sc_ref[h], v_ref[:, at(h)], (1, 0))
    wholes.finish()
    moving = []
    for unit in units:
        out[unit].finish()
        state = jnp.zeros((span, size), F32)
        for part in range(depth):
            zo[unit, part] = state
            state = jnp.exp(tzr[part, unit:unit + 1]) * state + zrb[unit, part]
        moving.append(over_z(zo.at[unit], zi.at[unit], 1 + own + unit))
    for h in in_order:
        qd_ref[:, at(h)] = (q_ref[:, at(h)].astype(F32) * row_scale[:, h:h + 1]).astype(BF16)
        u_ref[:, at(h)] = cot_ref[:, at(h)].astype(F32) * gain_ref[:, at(h)]
    out = []
    for unit in units:
        moving[unit].finish()
        state = zi[unit].reshape(size, size)
        for part in range(SIDE):
            yo[unit, part] = state
            if part < SIDE - 1:
                state = own_decay(part, unit) * state + yrb[unit, part]
        out.append(over_y(yo.at[unit], yi.at[unit], 1 + own + unit))

    squares = jnp.zeros((tokens, size), F32)
    slopes = jnp.zeros((tokens, size), F32)
    for unit in units:
        out[unit].finish()
        for part in range(SIDE):
            h = part * own + unit
            state = yi[unit, part].astype(BF16)
            s_ref[h] = state
            o = o_ref[:, at(h)] + dot(qd_ref[:, at(h)], state, (1, 0))
            o_ref[:, at(h)] = o
            squares = squares + o * o
            slopes = slopes + u_ref[:, at(h)] * o
    hs[0:1] = jnp.sum(jnp.transpose(squares), axis=0, keepdims=True)
    hs[1:2] = jnp.sum(jnp.transpose(slopes), axis=0, keepdims=True)
    exchange(hs, hr, (hs_sem, hr_sem), 0, head, group, h_peer, True).finish()
    both = hr[0]
    for part in range(1, group):
        both = both + hr[part]
    inverse_row = lax.rsqrt(both[0:1] / features + EPSILON)
    pull_row = inverse_row * inverse_row * (inverse_row * both[1:2]) / features
    inverse = jnp.transpose(jnp.broadcast_to(inverse_row, (size, tokens)))
    pull = jnp.transpose(jnp.broadcast_to(pull_row, (size, tokens)))

    first = 1 + 2 * own
    moving = []
    for unit in units:
        for part in range(SIDE):
            h = part * own + unit
            do = (inverse * u_ref[:, at(h)] - o_ref[:, at(h)] * pull).astype(BF16)
            do_ref[:, at(h)] = do
            yb2[unit, part] = dot(qd_ref[:, at(h)], do, (0, 0))
        moving.append(over_y(yb2.at[unit], yrb2.at[unit], first + unit))
    for h in in_order:
        ds_ref[h] = (dot(do_ref[:, at(h)], v_ref[:, at(h)], (1, 1)) * w_ref[h]).astype(BF16)
    out = []
    for unit in units:
        moving[unit].finish()
        state = yrb2[unit, SIDE - 1]
        for part in reversed(range(SIDE - 1)):
            state = own_decay(part, unit) * state + yrb2[unit, part]
        zb2[unit] = state.reshape(depth, span, size)
        out.append(over_z(zb2.at[unit], zrb2.at[unit], first + unit))
    for h in in_order:
        normed_ref[:, at(h)] = (o_ref[:, at(h)] * inverse * gain_ref[:, at(h)]).astype(BF16)
        gq_ref[:, at(h)] = (
            dot(ds_ref[h], k_ref[:, at(h)], (1, 0))
            + dot(do_ref[:, at(h)], s_ref[h], (1, 1)) * row_scale[:, h:h + 1]
        ).astype(BF16)
    moving = []
    for unit in units:
        out[unit].finish()
        state = jnp.zeros((span, size), F32)
        for part in reversed(range(depth)):
            zo2[unit, part] = state
            state = jnp.exp(tzr[part, unit:unit + 1]) * state + zrb2[unit, part]
        moving.append(over_z(zo2.at[unit], zi2.at[unit], first + own + unit))
    for h in in_order:
        gkl_ref[:, at(h)] = dot(ds_ref[h], q_ref[:, at(h)], (0, 0))
        gvl_ref[:, at(h)] = dot(sc_ref[h], do_ref[:, at(h)], (0, 0))
    out = []
    for unit in units:
        moving[unit].finish()
        state = zi2[unit].reshape(size, size)
        for part in reversed(range(SIDE)):
            yo2[unit, part] = state
            if part > 0:
                state = own_decay(part, unit) * state + yrb2[unit, part]
        out.append(over_y(yo2.at[unit], yi2.at[unit], first + own + unit))
    for unit in units:
        out[unit].finish()
        for part in range(SIDE):
            h = part * own + unit
            state = yi2[unit, part].astype(BF16)
            gk_ref[:, at(h)] = (
                gkl_ref[:, at(h)] + dot(v_ref[:, at(h)], state, (1, 1)) * tail[:, h:h + 1]
            ).astype(BF16)
            gv_ref[:, at(h)] = (
                gvl_ref[:, at(h)] + dot(kd_ref[:, at(h)], state, (1, 0))
            ).astype(BF16)
    for made in exchanges:
        made.drain()


def per_device(queries, keys, values, log_decay, gain, cotangent):
    tokens, width = queries.shape
    heads = log_decay.shape[1]
    size = width // heads
    seq_count, group = lax.axis_size("seq"), lax.axis_size("head")
    depth = seq_count // SIDE
    own = heads // SIDE
    block = pl.BlockSpec(memory_space=pltpu.VMEM)
    square = (heads, tokens, tokens)
    flat = (tokens, width)
    V = pltpu.VMEM
    Sem = pltpu.SemaphoreType.DMA
    y_slots = V((own, SIDE, size, size), F32)
    z_slots = V((own, depth, size // depth, size), F32)
    way = [y_slots, y_slots, z_slots, z_slots, z_slots, z_slots, y_slots, y_slots]
    steps = 1 + 4 * own
    out = jax.ShapeDtypeStruct(flat, BF16)
    return pl.pallas_call(
        functools.partial(kernel, seq_count, group, float(width * group)),
        out_shape=(out, out, out, out),
        in_specs=[block] * 6,
        out_specs=(block,) * 4,
        scratch_shapes=[
            V(square, F32), V(square, BF16), V(square, BF16),
            V(flat, F32), V(flat, F32), V(flat, F32), V(flat, F32),
            V(flat, BF16), V(flat, BF16), V(flat, BF16),
            V((heads, size, size), BF16),
            *way, *way,
            V((SIDE, own, size), F32), V((SIDE, own, size), F32),
            V((own, size), F32), V((depth, own, size), F32),
            V((2, tokens), F32), V((group, 2, tokens), F32),
            Sem((steps, SIDE)), Sem((steps, SIDE)),
            Sem((steps, depth)), Sem((steps, depth)),
            Sem((1, group)), Sem((1, group)),
        ],
        compiler_params=pltpu.CompilerParams(collective_id=0, has_side_effects=True),
        name="attention_both_ways",
    )(queries, keys, values, log_decay.T, gain.reshape(1, width), cotangent)


def solution(mesh):
    placed = (
        P("seq", "head"),
        P("seq", "head"),
        P("seq", "head"),
        P("seq", "head"),
        P("head"),
        P("seq", "head"),
    )
    return jax.shard_map(
        per_device,
        mesh=mesh,
        in_specs=placed,
        out_specs=(P("seq", "head"), P("seq", "head"), P("seq", "head"), P("seq", "head")),
        check_vma=False,
    )
```

```python
import functools

import jax
import jax.numpy as jnp
from jax import lax
from jax.experimental import pallas as pl
from jax.experimental.pallas import tpu as pltpu
from jax.sharding import PartitionSpec as P

EPSILON = 1e-05
SIDE = 4
CUT = 1
F32 = jnp.float32
BF16 = jnp.bfloat16
HIGHEST = lax.Precision.HIGHEST


def dot(a, b, contract, precision=None):
    return lax.dot_general(
        a, b, ((contract[:1], contract[1:]), ((), ())), precision=precision,
        preferred_element_type=F32,
    )


def exchange_order(count):
    return sorted(range(1, count), key=lambda d: -min(d, count - d))


class Exchange:
    def __init__(self, source, target, send_sem, recv_sem, place, count, device, shared=False):
        self.source, self.target, self.place, self.count = source, target, place, count
        self.send_sem, self.recv_sem, self.device, self.shared = send_sem, recv_sem, device, shared
        self.started = []

    def copy(self, peer, slot, step):
        return pltpu.make_async_remote_copy(
            src_ref=self.source if self.shared else self.source.at[peer],
            dst_ref=self.target.at[slot],
            send_sem=self.send_sem.at[step],
            recv_sem=self.recv_sem.at[step],
            device_id=self.device(peer),
            device_id_type=pl.DeviceIdType.MESH,
        )

    def start(self):
        for step in exchange_order(self.count):
            copy = self.copy(lax.rem(self.place + step, self.count), self.place, step)
            copy.start()
            self.started.append(copy)
        self.target[self.place] = self.source[...] if self.shared else self.source[self.place]

    def finish(self):
        for step in range(1, self.count):
            peer = lax.rem(self.place + self.count - step, self.count)
            self.copy(peer, peer, step).wait_recv()

    def drain(self):
        for copy in self.started:
            copy.wait_send()


def kernel(
    seq_count, group, features,
    q_in, k_in, v_in, ld_in, gain_in, cot_in,
    normed_ref, gq_ref, gk_ref, gv_ref,
    w_ref, sc_ref, ds_ref, o_ref, u_ref, gkl_ref, gvl_ref, qd_ref, kd_ref, do_ref, s_ref,
    yb, yrb, zb, zrb, zo, zi, yo, yi,
    yb2, yrb2, zb2, zrb2, zo2, zi2, yo2, yi2,
    tb, trb, tz, tzr, hs, hr,
    ys, yr, zs, zr, hs_sem, hr_sem,
    q_ref, k_ref, v_ref, ld_ref, gain_ref, cot_ref, in_sem,
):
    loads = [
        pltpu.make_async_copy(source, target, in_sem.at[i])
        for i, (source, target) in enumerate((
            (ld_in, ld_ref), (k_in, k_ref), (v_in, v_ref),
            (q_in, q_ref), (cot_in, cot_ref), (gain_in, gain_ref),
        ))
    ]
    tokens = q_ref.shape[0]
    heads = ld_ref.shape[0]
    size = q_ref.shape[1] // heads
    depth = seq_count // SIDE
    own = heads // SIDE
    rows = size // CUT
    span = rows // depth
    scaling = size ** (-0.5)
    seq, head = lax.axis_index("seq"), lax.axis_index("head")
    z, y = seq // SIDE, lax.rem(seq, SIDE)

    def y_peer(p):
        return (z * SIDE + p, head)

    def z_peer(p):
        return (p * SIDE + y, head)

    def h_peer(p):
        return (seq, p)

    barrier = pltpu.get_barrier_semaphore()
    for place, count, device in ((z, depth, z_peer), (y, SIDE, y_peer), (head, group, h_peer)):
        for step in exchange_order(count):
            pl.semaphore_signal(
                barrier, inc=1, device_id=device(lax.rem(place + step, count)),
                device_id_type=pl.DeviceIdType.MESH,
            )

    for load in loads:
        load.start()
    exchanges = []

    def exchange(source, target, sems, index, place, count, device, shared=False):
        made = Exchange(
            source, target, sems[0].at[index], sems[1].at[index], place, count, device, shared
        )
        made.start()
        exchanges.append(made)
        return made

    def over_y(source, target, index, shared=False):
        return exchange(source, target, (ys, yr), index, y, SIDE, y_peer, shared)

    def over_z(source, target, index, shared=False):
        return exchange(source, target, (zs, zr), index, z, depth, z_peer, shared)

    def at(h):
        return slice(h * size, (h + 1) * size)

    units = range(own * CUT)
    in_order = [part * own + place for place in range(own) for part in range(SIDE)]

    def put(slots, h, value):
        for piece in range(CUT):
            slots[h % own * CUT + piece, h // own] = value[piece * rows:(piece + 1) * rows]

    row = lax.broadcasted_iota(jnp.int32, (tokens, tokens), 0)
    column = lax.broadcasted_iota(jnp.int32, (tokens, tokens), 1)
    causal = row >= column
    lower = jnp.where(causal, 1.0, 0.0).astype(F32)
    loads[0].wait()
    log_decay = ld_ref[...]
    c = dot(lower, log_decay, (1, 1), HIGHEST)
    c_rows = dot(log_decay, lower, (1, 1), HIGHEST)
    total = jnp.broadcast_to(c_rows[:, tokens - 1:tokens], (heads, size))
    for part in range(SIDE):
        tb[part] = total[part * own:(part + 1) * own]
    tail = jnp.exp(c[tokens - 1:tokens, :] - c)
    row_scale = scaling * jnp.exp(c)

    loads[1].wait()
    loads[2].wait()
    for h in in_order:
        kd = (k_ref[:, at(h)].astype(F32) * tail[:, h:h + 1]).astype(BF16)
        kd_ref[:, at(h)] = kd
        put(yb, h, dot(kd, v_ref[:, at(h)], (0, 0)))
    for load in loads[3:]:
        load.wait()
    pl.semaphore_wait(barrier, SIDE + depth + group - 3)

    totals = over_y(tb, trb, 0)
    moving = [over_y(yb.at[unit], yrb.at[unit], 1 + unit) for unit in units]
    totals.finish()
    whole = trb[0]
    for part in range(1, SIDE):
        whole = whole + trb[part]
    tz[...] = whole
    wholes = over_z(tz, tzr, 0, True)

    def own_decay(part, unit):
        return jnp.exp(trb[part, unit // CUT:unit // CUT + 1])

    for h in in_order:
        gaps = c[:, h:h + 1] - c_rows[h:h + 1, :]
        weights = jnp.where(causal, jnp.exp(jnp.where(causal, gaps, 0.0)), 0.0) * scaling
        w_ref[h] = weights
        sc_ref[h] = (dot(q_ref[:, at(h)], k_ref[:, at(h)], (1, 1)) * weights).astype(BF16)
    out = []
    for unit in units:
        moving[unit].finish()
        state = yrb[unit, 0]
        for part in range(1, SIDE):
            state = own_decay(part, unit) * state + yrb[unit, part]
        zb[unit] = state.reshape(depth, span, size)
        out.append(over_z(zb.at[unit], zrb.at[unit], 1 + unit))
    for h in in_order:
        o_ref[:, at(h)] = dot(sc_ref[h], v_ref[:, at(h)], (1, 0))
    wholes.finish()
    moving = []
    for unit in units:
        out[unit].finish()
        state = jnp.zeros((span, size), F32)
        for part in range(depth):
            zo[unit, part] = state
            state = jnp.exp(tzr[part, unit // CUT:unit // CUT + 1]) * state + zrb[unit, part]
        moving.append(over_z(zo.at[unit], zi.at[unit], 1 + len(units) + unit))
    for h in in_order:
        qd_ref[:, at(h)] = (q_ref[:, at(h)].astype(F32) * row_scale[:, h:h + 1]).astype(BF16)
        u_ref[:, at(h)] = cot_ref[:, at(h)].astype(F32) * gain_ref[:, at(h)]
    out = []
    for unit in units:
        moving[unit].finish()
        state = zi[unit].reshape(rows, size)
        for part in range(SIDE):
            yo[unit, part] = state
            if part < SIDE - 1:
                state = own_decay(part, unit) * state + yrb[unit, part]
        out.append(over_y(yo.at[unit], yi.at[unit], 1 + len(units) + unit))

    squares = jnp.zeros((tokens, size), F32)
    slopes = jnp.zeros((tokens, size), F32)
    for place in range(own):
        pieces = range(place * CUT, (place + 1) * CUT)
        for unit in pieces:
            out[unit].finish()
        for part in range(SIDE):
            h = part * own + place
            state = jnp.concatenate([yi[unit, part] for unit in pieces], axis=0).astype(BF16)
            s_ref[h] = state
            o = o_ref[:, at(h)] + dot(qd_ref[:, at(h)], state, (1, 0))
            o_ref[:, at(h)] = o
            squares = squares + o * o
            slopes = slopes + u_ref[:, at(h)] * o
    hs[0:1] = jnp.sum(jnp.transpose(squares), axis=0, keepdims=True)
    hs[1:2] = jnp.sum(jnp.transpose(slopes), axis=0, keepdims=True)
    exchange(hs, hr, (hs_sem, hr_sem), 0, head, group, h_peer, True).finish()
    both = hr[0]
    for part in range(1, group):
        both = both + hr[part]
    inverse_row = lax.rsqrt(both[0:1] / features + EPSILON)
    pull_row = inverse_row * inverse_row * (inverse_row * both[1:2]) / features
    inverse = jnp.transpose(jnp.broadcast_to(inverse_row, (size, tokens)))
    pull = jnp.transpose(jnp.broadcast_to(pull_row, (size, tokens)))

    first = 1 + 2 * len(units)
    moving = []
    for place in range(own):
        for part in range(SIDE):
            h = part * own + place
            do = (inverse * u_ref[:, at(h)] - o_ref[:, at(h)] * pull).astype(BF16)
            do_ref[:, at(h)] = do
            put(yb2, h, dot(qd_ref[:, at(h)], do, (0, 0)))
        for unit in range(place * CUT, (place + 1) * CUT):
            moving.append(over_y(yb2.at[unit], yrb2.at[unit], first + unit))
    for h in in_order:
        ds_ref[h] = (dot(do_ref[:, at(h)], v_ref[:, at(h)], (1, 1)) * w_ref[h]).astype(BF16)
    out = []
    for unit in units:
        moving[unit].finish()
        state = yrb2[unit, SIDE - 1]
        for part in reversed(range(SIDE - 1)):
            state = own_decay(part, unit) * state + yrb2[unit, part]
        zb2[unit] = state.reshape(depth, span, size)
        out.append(over_z(zb2.at[unit], zrb2.at[unit], first + unit))
    for h in in_order:
        normed_ref[:, at(h)] = (o_ref[:, at(h)] * inverse * gain_ref[:, at(h)]).astype(BF16)
        gq_ref[:, at(h)] = (
            dot(ds_ref[h], k_ref[:, at(h)], (1, 0))
            + dot(do_ref[:, at(h)], s_ref[h], (1, 1)) * row_scale[:, h:h + 1]
        ).astype(BF16)
    moving = []
    for unit in units:
        out[unit].finish()
        state = jnp.zeros((span, size), F32)
        for part in reversed(range(depth)):
            zo2[unit, part] = state
            state = jnp.exp(tzr[part, unit // CUT:unit // CUT + 1]) * state + zrb2[unit, part]
        moving.append(over_z(zo2.at[unit], zi2.at[unit], first + len(units) + unit))
    for h in in_order:
        gkl_ref[:, at(h)] = dot(ds_ref[h], q_ref[:, at(h)], (0, 0))
        gvl_ref[:, at(h)] = dot(sc_ref[h], do_ref[:, at(h)], (0, 0))
    out = []
    for unit in units:
        moving[unit].finish()
        state = zi2[unit].reshape(rows, size)
        for part in reversed(range(SIDE)):
            yo2[unit, part] = state
            if part > 0:
                state = own_decay(part, unit) * state + yrb2[unit, part]
        out.append(over_y(yo2.at[unit], yi2.at[unit], first + len(units) + unit))
    for place in range(own):
        pieces = range(place * CUT, (place + 1) * CUT)
        for unit in pieces:
            out[unit].finish()
        for part in range(SIDE):
            h = part * own + place
            state = jnp.concatenate([yi2[unit, part] for unit in pieces], axis=0).astype(BF16)
            gk_ref[:, at(h)] = (
                gkl_ref[:, at(h)] + dot(v_ref[:, at(h)], state, (1, 1)) * tail[:, h:h + 1]
            ).astype(BF16)
            gv_ref[:, at(h)] = (
                gvl_ref[:, at(h)] + dot(kd_ref[:, at(h)], state, (1, 0))
            ).astype(BF16)
    for made in exchanges:
        made.drain()


def hand_on(*refs):
    for source, target in zip(refs[:4], refs[4:]):
        target[...] = source[...]


def per_device(queries, keys, values, log_decay, gain, cotangent):
    tokens, width = queries.shape
    heads = log_decay.shape[1]
    size = width // heads
    seq_count, group = lax.axis_size("seq"), lax.axis_size("head")
    depth = seq_count // SIDE
    own = heads // SIDE
    block = pl.BlockSpec(memory_space=pltpu.VMEM)
    square = (heads, tokens, tokens)
    flat = (tokens, width)
    V = pltpu.VMEM
    Sem = pltpu.SemaphoreType.DMA
    count = own * CUT
    rows = size // CUT
    y_slots = V((count, SIDE, rows, size), F32)
    z_slots = V((count, depth, rows // depth, size), F32)
    way = [y_slots, y_slots, z_slots, z_slots, z_slots, z_slots, y_slots, y_slots]
    steps = 1 + 4 * count
    out = jax.ShapeDtypeStruct(flat, BF16)
    results = pl.pallas_call(
        functools.partial(kernel, seq_count, group, float(width * group)),
        out_shape=(out, out, out, out),
        in_specs=[pl.BlockSpec(memory_space=pl.ANY)] * 6,
        out_specs=(block,) * 4,
        scratch_shapes=[
            V(square, F32), V(square, BF16), V(square, BF16),
            V(flat, F32), V(flat, F32), V(flat, F32), V(flat, F32),
            V(flat, BF16), V(flat, BF16), V(flat, BF16),
            V((heads, size, size), BF16),
            *way, *way,
            V((SIDE, own, size), F32), V((SIDE, own, size), F32),
            V((own, size), F32), V((depth, own, size), F32),
            V((2, tokens), F32), V((group, 2, tokens), F32),
            Sem((steps, SIDE)), Sem((steps, SIDE)),
            Sem((steps, depth)), Sem((steps, depth)),
            Sem((1, group)), Sem((1, group)),
            V(flat, BF16), V(flat, BF16), V(flat, BF16),
            V((heads, tokens), F32), V((1, width), F32), V(flat, BF16), Sem((6,)),
        ],
        compiler_params=pltpu.CompilerParams(collective_id=0, has_side_effects=True),
        name="attention_both_ways",
    )(queries, keys, values, log_decay.T, gain.reshape(1, width), cotangent)
    tile = pl.BlockSpec((tokens // 1, width), lambda i: (i, 0))
    return pl.pallas_call(
        hand_on,
        grid=(1,),
        out_shape=(out, out, out, out),
        in_specs=[tile] * 4,
        out_specs=(tile,) * 4,
        name="hand_on",
    )(*results)


def solution(mesh):
    placed = (
        P("seq", "head"),
        P("seq", "head"),
        P("seq", "head"),
        P("seq", "head"),
        P("head"),
        P("seq", "head"),
    )
    return jax.shard_map(
        per_device,
        mesh=mesh,
        in_specs=placed,
        out_specs=(P("seq", "head"), P("seq", "head"), P("seq", "head"), P("seq", "head")),
        check_vma=False,
    )
```

```python
import functools

import jax
import jax.numpy as jnp
from jax import lax
from jax.experimental import pallas as pl
from jax.experimental.pallas import tpu as pltpu
from jax.sharding import PartitionSpec as P

EPSILON = 1e-05
SIDE = 4
CUT = 1
F32 = jnp.float32
BF16 = jnp.bfloat16
HIGHEST = lax.Precision.HIGHEST


def dot(a, b, contract, precision=None):
    return lax.dot_general(
        a, b, ((contract[:1], contract[1:]), ((), ())), precision=precision,
        preferred_element_type=F32,
    )


def exchange_order(count):
    return sorted(range(1, count), key=lambda d: -min(d, count - d))


class Exchange:
    def __init__(self, source, target, send_sem, recv_sem, place, count, device, shared=False):
        self.source, self.target, self.place, self.count = source, target, place, count
        self.send_sem, self.recv_sem, self.device, self.shared = send_sem, recv_sem, device, shared
        self.started = []

    def copy(self, peer, slot, step):
        return pltpu.make_async_remote_copy(
            src_ref=self.source if self.shared else self.source.at[peer],
            dst_ref=self.target.at[slot],
            send_sem=self.send_sem.at[step],
            recv_sem=self.recv_sem.at[step],
            device_id=self.device(peer),
            device_id_type=pl.DeviceIdType.MESH,
        )

    def start(self):
        for step in exchange_order(self.count):
            copy = self.copy(lax.rem(self.place + step, self.count), self.place, step)
            copy.start()
            self.started.append(copy)
        self.target[self.place] = self.source[...] if self.shared else self.source[self.place]

    def finish(self):
        for step in range(1, self.count):
            peer = lax.rem(self.place + self.count - step, self.count)
            self.copy(peer, peer, step).wait_recv()

    def drain(self):
        for copy in self.started:
            copy.wait_send()


def kernel(
    seq_count, group, features,
    q_in, k_in, v_in, ld_in, gain_in, cot_in,
    normed_ref, gq_ref, gk_ref, gv_ref,
    w_ref, sc_ref, ds_ref, o_ref, u_ref, gkl_ref, gvl_ref, qd_ref, kd_ref, do_ref, s_ref,
    yb, yrb, zb, zrb, zo, zi, yo, yi,
    yb2, yrb2, zb2, zrb2, zo2, zi2, yo2, yi2,
    tb, trb, tz, tzr, hs, hr,
    ys, yr, zs, zr, hs_sem, hr_sem,
    q_ref, k_ref, v_ref, ld_ref, gain_ref, cot_ref, in_sem,
):
    loads = [
        pltpu.make_async_copy(source, target, in_sem.at[i])
        for i, (source, target) in enumerate((
            (ld_in, ld_ref), (k_in, k_ref), (v_in, v_ref),
            (q_in, q_ref), (cot_in, cot_ref), (gain_in, gain_ref),
        ))
    ]
    tokens = q_ref.shape[0]
    heads = ld_ref.shape[0]
    size = q_ref.shape[1] // heads
    depth = seq_count // SIDE
    own = heads // SIDE
    rows = size // CUT
    span = rows // depth
    scaling = size ** (-0.5)
    seq, head = lax.axis_index("seq"), lax.axis_index("head")
    z, y = seq // SIDE, lax.rem(seq, SIDE)

    def y_peer(p):
        return (z * SIDE + p, head)

    def z_peer(p):
        return (p * SIDE + y, head)

    def h_peer(p):
        return (seq, p)

    barrier = pltpu.get_barrier_semaphore()
    for place, count, device in ((z, depth, z_peer), (y, SIDE, y_peer), (head, group, h_peer)):
        for step in exchange_order(count):
            pl.semaphore_signal(
                barrier, inc=1, device_id=device(lax.rem(place + step, count)),
                device_id_type=pl.DeviceIdType.MESH,
            )

    for load in loads:
        load.start()
    exchanges = []

    def exchange(source, target, sems, index, place, count, device, shared=False):
        made = Exchange(
            source, target, sems[0].at[index], sems[1].at[index], place, count, device, shared
        )
        made.start()
        exchanges.append(made)
        return made

    def over_y(source, target, index, shared=False):
        return exchange(source, target, (ys, yr), index, y, SIDE, y_peer, shared)

    def over_z(source, target, index, shared=False):
        return exchange(source, target, (zs, zr), index, z, depth, z_peer, shared)

    def at(h):
        return slice(h * size, (h + 1) * size)

    units = range(own * CUT)
    in_order = [part * own + place for place in range(own) for part in range(SIDE)]

    def put(slots, h, value):
        for piece in range(CUT):
            slots[h % own * CUT + piece, h // own] = value[piece * rows:(piece + 1) * rows]

    row = lax.broadcasted_iota(jnp.int32, (tokens, tokens), 0)
    column = lax.broadcasted_iota(jnp.int32, (tokens, tokens), 1)
    causal = row >= column
    lower = jnp.where(causal, 1.0, 0.0).astype(F32)
    loads[0].wait()
    log_decay = ld_ref[...]
    c = dot(lower, log_decay, (1, 1), HIGHEST)
    c_rows = dot(log_decay, lower, (1, 1), HIGHEST)
    total = jnp.broadcast_to(c_rows[:, tokens - 1:tokens], (heads, size))
    for part in range(SIDE):
        tb[part] = total[part * own:(part + 1) * own]
    tail = jnp.exp(c[tokens - 1:tokens, :] - c)
    row_scale = scaling * jnp.exp(c)

    loads[1].wait()
    loads[2].wait()
    for h in in_order:
        kd = (k_ref[:, at(h)].astype(F32) * tail[:, h:h + 1]).astype(BF16)
        kd_ref[:, at(h)] = kd
        put(yb, h, dot(kd, v_ref[:, at(h)], (0, 0)))
    for load in loads[3:]:
        load.wait()
    pl.semaphore_wait(barrier, SIDE + depth + group - 3)

    totals = over_y(tb, trb, 0)
    moving = [over_y(yb.at[unit], yrb.at[unit], 1 + unit) for unit in units]
    totals.finish()
    whole = trb[0]
    for part in range(1, SIDE):
        whole = whole + trb[part]
    tz[...] = whole
    wholes = over_z(tz, tzr, 0, True)

    def own_decay(part, unit):
        return jnp.exp(trb[part, unit // CUT:unit // CUT + 1])

    for h in in_order:
        qd_ref[:, at(h)] = (q_ref[:, at(h)].astype(F32) * row_scale[:, h:h + 1]).astype(BF16)
        u_ref[:, at(h)] = cot_ref[:, at(h)].astype(F32) * gain_ref[:, at(h)]
    out = []
    for unit in units:
        moving[unit].finish()
        state = yrb[unit, 0]
        for part in range(1, SIDE):
            state = own_decay(part, unit) * state + yrb[unit, part]
        zb[unit] = state.reshape(depth, span, size)
        out.append(over_z(zb.at[unit], zrb.at[unit], 1 + unit))
    for h in in_order:
        gaps = c[:, h:h + 1] - c_rows[h:h + 1, :]
        weights = jnp.where(causal, jnp.exp(jnp.where(causal, gaps, 0.0)), 0.0) * scaling
        w_ref[h] = weights
        sc_ref[h] = (dot(q_ref[:, at(h)], k_ref[:, at(h)], (1, 1)) * weights).astype(BF16)
    wholes.finish()
    moving = []
    for unit in units:
        out[unit].finish()
        state = jnp.zeros((span, size), F32)
        for part in range(depth):
            zo[unit, part] = state
            state = jnp.exp(tzr[part, unit // CUT:unit // CUT + 1]) * state + zrb[unit, part]
        moving.append(over_z(zo.at[unit], zi.at[unit], 1 + len(units) + unit))
    for h in in_order:
        o_ref[:, at(h)] = dot(sc_ref[h], v_ref[:, at(h)], (1, 0))
    out = []
    for unit in units:
        moving[unit].finish()
        state = zi[unit].reshape(rows, size)
        for part in range(SIDE):
            yo[unit, part] = state
            if part < SIDE - 1:
                state = own_decay(part, unit) * state + yrb[unit, part]
        out.append(over_y(yo.at[unit], yi.at[unit], 1 + len(units) + unit))

    squares = jnp.zeros((tokens, size), F32)
    slopes = jnp.zeros((tokens, size), F32)
    for place in range(own):
        pieces = range(place * CUT, (place + 1) * CUT)
        for unit in pieces:
            out[unit].finish()
        for part in range(SIDE):
            h = part * own + place
            state = jnp.concatenate([yi[unit, part] for unit in pieces], axis=0).astype(BF16)
            s_ref[h] = state
            o = o_ref[:, at(h)] + dot(qd_ref[:, at(h)], state, (1, 0))
            o_ref[:, at(h)] = o
            squares = squares + o * o
            slopes = slopes + u_ref[:, at(h)] * o
    hs[0:1] = jnp.sum(jnp.transpose(squares), axis=0, keepdims=True)
    hs[1:2] = jnp.sum(jnp.transpose(slopes), axis=0, keepdims=True)
    exchange(hs, hr, (hs_sem, hr_sem), 0, head, group, h_peer, True).finish()
    both = hr[0]
    for part in range(1, group):
        both = both + hr[part]
    inverse_row = lax.rsqrt(both[0:1] / features + EPSILON)
    pull_row = inverse_row * inverse_row * (inverse_row * both[1:2]) / features
    inverse = jnp.transpose(jnp.broadcast_to(inverse_row, (size, tokens)))
    pull = jnp.transpose(jnp.broadcast_to(pull_row, (size, tokens)))

    first = 1 + 2 * len(units)
    moving = []
    for place in range(own):
        for part in range(SIDE):
            h = part * own + place
            do = (inverse * u_ref[:, at(h)] - o_ref[:, at(h)] * pull).astype(BF16)
            do_ref[:, at(h)] = do
            put(yb2, h, dot(qd_ref[:, at(h)], do, (0, 0)))
        for unit in range(place * CUT, (place + 1) * CUT):
            moving.append(over_y(yb2.at[unit], yrb2.at[unit], first + unit))
    for h in in_order:
        normed_ref[:, at(h)] = (o_ref[:, at(h)] * inverse * gain_ref[:, at(h)]).astype(BF16)
    out = []
    for unit in units:
        moving[unit].finish()
        state = yrb2[unit, SIDE - 1]
        for part in reversed(range(SIDE - 1)):
            state = own_decay(part, unit) * state + yrb2[unit, part]
        zb2[unit] = state.reshape(depth, span, size)
        out.append(over_z(zb2.at[unit], zrb2.at[unit], first + unit))
    for h in in_order:
        ds_ref[h] = (dot(do_ref[:, at(h)], v_ref[:, at(h)], (1, 1)) * w_ref[h]).astype(BF16)
    for h in in_order:
        gq_ref[:, at(h)] = (
            dot(ds_ref[h], k_ref[:, at(h)], (1, 0))
            + dot(do_ref[:, at(h)], s_ref[h], (1, 1)) * row_scale[:, h:h + 1]
        ).astype(BF16)
    moving = []
    for unit in units:
        out[unit].finish()
        state = jnp.zeros((span, size), F32)
        for part in reversed(range(depth)):
            zo2[unit, part] = state
            state = jnp.exp(tzr[part, unit // CUT:unit // CUT + 1]) * state + zrb2[unit, part]
        moving.append(over_z(zo2.at[unit], zi2.at[unit], first + len(units) + unit))
    for h in in_order:
        gkl_ref[:, at(h)] = dot(ds_ref[h], q_ref[:, at(h)], (0, 0))
        gvl_ref[:, at(h)] = dot(sc_ref[h], do_ref[:, at(h)], (0, 0))
    out = []
    for unit in units:
        moving[unit].finish()
        state = zi2[unit].reshape(rows, size)
        for part in reversed(range(SIDE)):
            yo2[unit, part] = state
            if part > 0:
                state = own_decay(part, unit) * state + yrb2[unit, part]
        out.append(over_y(yo2.at[unit], yi2.at[unit], first + len(units) + unit))
    for place in range(own):
        pieces = range(place * CUT, (place + 1) * CUT)
        for unit in pieces:
            out[unit].finish()
        for part in range(SIDE):
            h = part * own + place
            state = jnp.concatenate([yi2[unit, part] for unit in pieces], axis=0).astype(BF16)
            gk_ref[:, at(h)] = (
                gkl_ref[:, at(h)] + dot(v_ref[:, at(h)], state, (1, 1)) * tail[:, h:h + 1]
            ).astype(BF16)
            gv_ref[:, at(h)] = (
                gvl_ref[:, at(h)] + dot(kd_ref[:, at(h)], state, (1, 0))
            ).astype(BF16)
    for made in exchanges:
        made.drain()


def hand_on(*refs):
    for source, target in zip(refs[:4], refs[4:]):
        target[...] = source[...]


def per_device(queries, keys, values, log_decay, gain, cotangent):
    tokens, width = queries.shape
    heads = log_decay.shape[1]
    size = width // heads
    seq_count, group = lax.axis_size("seq"), lax.axis_size("head")
    depth = seq_count // SIDE
    own = heads // SIDE
    block = pl.BlockSpec(memory_space=pltpu.VMEM)
    square = (heads, tokens, tokens)
    flat = (tokens, width)
    V = pltpu.VMEM
    Sem = pltpu.SemaphoreType.DMA
    count = own * CUT
    rows = size // CUT
    y_slots = V((count, SIDE, rows, size), F32)
    z_slots = V((count, depth, rows // depth, size), F32)
    way = [y_slots, y_slots, z_slots, z_slots, z_slots, z_slots, y_slots, y_slots]
    steps = 1 + 4 * count
    out = jax.ShapeDtypeStruct(flat, BF16)
    results = pl.pallas_call(
        functools.partial(kernel, seq_count, group, float(width * group)),
        out_shape=(out, out, out, out),
        in_specs=[pl.BlockSpec(memory_space=pl.ANY)] * 6,
        out_specs=(block,) * 4,
        scratch_shapes=[
            V(square, F32), V(square, BF16), V(square, BF16),
            V(flat, F32), V(flat, F32), V(flat, F32), V(flat, F32),
            V(flat, BF16), V(flat, BF16), V(flat, BF16),
            V((heads, size, size), BF16),
            *way, *way,
            V((SIDE, own, size), F32), V((SIDE, own, size), F32),
            V((own, size), F32), V((depth, own, size), F32),
            V((2, tokens), F32), V((group, 2, tokens), F32),
            Sem((steps, SIDE)), Sem((steps, SIDE)),
            Sem((steps, depth)), Sem((steps, depth)),
            Sem((1, group)), Sem((1, group)),
            V(flat, BF16), V(flat, BF16), V(flat, BF16),
            V((heads, tokens), F32), V((1, width), F32), V(flat, BF16), Sem((6,)),
        ],
        compiler_params=pltpu.CompilerParams(collective_id=0, has_side_effects=True),
        name="attention_both_ways",
    )(queries, keys, values, log_decay.T, gain.reshape(1, width), cotangent)
    tile = pl.BlockSpec((tokens // 1, width), lambda i: (i, 0))
    return pl.pallas_call(
        hand_on,
        grid=(1,),
        out_shape=(out, out, out, out),
        in_specs=[tile] * 4,
        out_specs=(tile,) * 4,
        name="hand_on",
    )(*results)


def solution(mesh):
    placed = (
        P("seq", "head"),
        P("seq", "head"),
        P("seq", "head"),
        P("seq", "head"),
        P("head"),
        P("seq", "head"),
    )
    return jax.shard_map(
        per_device,
        mesh=mesh,
        in_specs=placed,
        out_specs=(P("seq", "head"), P("seq", "head"), P("seq", "head"), P("seq", "head")),
        check_vma=False,
    )
```
